256 devices in a mesh: row: 32 (over x, y, core), depth: 8 (over z).
Axes of the slice: x: 4, y: 4, z: 8, core: 2. Of those that a mesh axis runs over, the one named last changes fastest.
Arguments:
- l_cores: float32 [64, 64, 384, 384], P('row', 'depth'), may hold values from -0.0390625 to 0.0390625
- l_bucket: int32 [64, 64], P('row', 'depth'), may hold values from 1 to 3
- present: int32 [64, 64], P('row', 'depth'), may hold values 0 or 1
- u_cores: float32 [64, 4, 384, 384], P('depth', None, 'row'), may hold values from -6 to 6
- u_bucket: int32 [64, 4], P('depth'), may hold values from 1 to 3
- diag_cores: float32 [64, 4, 384, 384], P('row', None, 'depth'), may hold values from -6 to 6
- pivot_inv: float32 [4, 384, 384], P(None, 'row'), may hold values from -0.3125 to 0.3125
- coupling: float32 [3, 384, 384], P(None, 'row'), may hold values from -0.21875 to 0.21875
Outputs:
- finished: float32 [64, 4, 384, 384], P('row', None, 'depth')
The draws below stay inside these ranges and needn't reach their ends.
Inputs may be any that keep to these rules, and one draw needn't show every extreme that they name: A lower tile's core rank is l_bucket * 128. An upper tile's core rank is u_bucket * 128. `present`: 1 marks a nonzero lower tile.
All inputs are finite; a program needn't handle non-finite values. No bound on the sum of `present` on one device may be relied on, other than what follows from the above.
Results may differ from the reference program's by a relative error of at most 0.0003.
Values sent between devices are 32-bit elements; how exact they have to be, the bound alone decides.
A program may use at most 128 MiB of HBM per device.

```python
import jax
import jax.numpy as jnp
from jax import lax

R = 384
COLS = 4
TROWS = 64
PIVOTS = 64


def place_ends(entries, stream_key, least, top_value):
    extent = entries.shape
    index_at = [jax.random.randint(jax.random.fold_in(stream_key, axis), (), 0, extent[axis]) for axis in range(len(extent))]
    entries = entries.at[tuple(index_at)].set(least)
    longest = extent.index(max(extent))
    index_at[longest] = (index_at[longest] + 1) % extent[longest]
    return entries.at[tuple(index_at)].set(top_value)


def shard_levels(key, extent, pieces, low, high):
    gain = 1.0
    for dim, blocks in pieces:
        steps = jax.random.uniform(jax.random.fold_in(jax.random.fold_in(key, 6), dim), (blocks,), jnp.float32, low / len(pieces), high / len(pieces))
        gain = gain * jnp.repeat(jnp.exp(steps), extent[dim] // blocks).reshape((-1,) + (1,) * (len(extent) - 1 - dim))
    return gain


def noise(key, extent, scale, limit, shards=(), kind=jnp.bfloat16):
    array = scale * jax.random.normal(key, extent, jnp.float32)
    if shards:
        array = array * shard_levels(key, extent, shards, -0.22, 0.18)
    return jnp.clip(array, -limit, limit).astype(kind)


def setup_inputs(seed: int = 0) -> dict:
    key_of = jax.random.split(jax.random.key(seed), 9)
    return {
        "l_cores": noise(key_of[0], (TROWS, PIVOTS, R, R), (R * PIVOTS) ** -0.5, 0.0390625, ((0, 32), (1, 8)), jnp.float32),
        "l_bucket": place_ends(jax.random.randint(key_of[1], (TROWS, PIVOTS), 1, 4), jax.random.fold_in(key_of[1], 1), 1, 3).astype(jnp.int32),
        "present": place_ends((jax.random.randint(key_of[2], (TROWS, PIVOTS), 0, 4) < 3).astype(jnp.int32), jax.random.fold_in(key_of[2], 1), 0, 1),
        "u_cores": noise(key_of[3], (PIVOTS, COLS, R, R), 1.0, 6.0, ((0, 8), (2, 32)), jnp.float32),
        "u_bucket": place_ends(jax.random.randint(key_of[4], (PIVOTS, COLS), 1, 4), jax.random.fold_in(key_of[4], 1), 1, 3).astype(jnp.int32),
        "diag_cores": noise(key_of[5], (TROWS, COLS, R, R), 1.0, 6.0, ((0, 32), (2, 8)), jnp.float32),
        "pivot_inv": noise(key_of[6], (COLS, R, R), R ** -0.5, 0.3125, ((1, 32),), jnp.float32),
        "coupling": noise(key_of[7], (COLS - 1, R, R), (2 * R) ** -0.5, 0.21875, ((1, 32),), jnp.float32),
    }


HIGH = lax.Precision.HIGHEST


def reference(l_cores, l_bucket, present, u_cores, u_bucket, diag_cores, pivot_inv, coupling):
    rank_step = R // 3
    positions = jnp.arange(R, dtype=jnp.int32)
    u_keep = (positions[None, None, :] < (u_bucket * rank_step)[:, :, None]).astype(jnp.float32)
    u_masked = u_cores * u_keep[..., None]

    def one_row(inputs):
        cores, buckets, flags, targets = inputs
        col_keep = ((positions[None, :] < (buckets * rank_step)[:, None]) & (flags[:, None] > 0)).astype(jnp.float32)
        masked = cores * col_keep[:, None, :]
        updates = jnp.einsum("kar,kjrb->jab", masked, u_masked, precision=HIGH)
        reduced = targets - updates
        previous = jnp.dot(reduced[0], pivot_inv[0], precision=HIGH, preferred_element_type=jnp.float32)
        results = [previous]
        for column in range(1, COLS):
            linked = jnp.dot(previous, coupling[column - 1], precision=HIGH, preferred_element_type=jnp.float32)
            previous = jnp.dot(reduced[column] - linked, pivot_inv[column], precision=HIGH, preferred_element_type=jnp.float32)
            results.append(previous)
        return jnp.stack(results)

    return lax.map(one_row, (l_cores, l_bucket, present, diag_cores))
```

```python
import jax
import jax.numpy as jnp
from jax import lax
from jax.experimental import pallas as pl
from jax.experimental.pallas import tpu as pltpu
from jax.sharding import PartitionSpec as P

MESH = pl.DeviceIdType.MESH
NX, NY, NZ = 4, 4, 8
R = 384
W = 256
CHUNKS = 6
PCH = CHUNKS
BF, F32 = jnp.bfloat16, jnp.float32


def split(a):
    hi = a.astype(BF)
    return hi, (a - hi.astype(F32)).astype(BF)


def dot(a, b):
    return jnp.dot(a, b, preferred_element_type=F32)


def kernel(
    lb, pr, ub, l_hbm, u_hbm, d_hbm, p_hbm, c_hbm,
    out,
    g, pg, h, hp, pc, ls, lhi, llo, acc, rb, red, diag,
    lsem, lssem, sib_s, sib_r, ag_s, ag_r, rs_s, rs_r,
):
    row = lax.axis_index("row")
    z = lax.axis_index("depth")
    x, y, c = row // 8, (row // 2) % 4, row % 2
    chip = x * 4 + y

    def dev(xx, yy, cc, zz):
        return ((xx * 4 + yy) * 2 + cc, zz)

    def wrap(v, n):
        return (v + n) % n

    sib = dev(x, y, 1 - c, z)
    near = {
        ("x", 1): dev(wrap(x + 1, NX), y, c, z), ("x", -1): dev(wrap(x - 1, NX), y, c, z),
        ("y", 1): dev(x, wrap(y + 1, NY), c, z), ("y", -1): dev(x, wrap(y - 1, NY), c, z),
        ("z", 1): dev(x, y, c, wrap(z + 1, NZ)), ("z", -1): dev(x, y, c, wrap(z - 1, NZ)),
    }

    sends = []

    def remote(src, dst, ssem, rsem, to):
        return pltpu.make_async_remote_copy(
            src_ref=src, dst_ref=dst, send_sem=ssem, recv_sem=rsem, device_id=to, device_id_type=MESH
        )

    def send(src, dst, ssem, rsem, to):
        copy = remote(src, dst, ssem, rsem, to)
        copy.start()
        sends.append(copy)

    def load_l(k):
        return pltpu.make_async_copy(l_hbm.at[:, k], ls.at[k % 2], lssem.at[k % 2])

    own_u = pltpu.make_async_copy(u_hbm.at[pl.ds(4 * c, 4)], h.at[c], lsem.at[0])
    own_p = pltpu.make_async_copy(p_hbm, pc.at[pl.ds(0, 4)], lsem.at[1])
    own_c = pltpu.make_async_copy(c_hbm, pc.at[pl.ds(4, 3)], lsem.at[2])
    own_d = pltpu.make_async_copy(d_hbm, diag, lsem.at[3])
    own_u.start()
    load_l(0).start()
    load_l(1).start()
    own_p.start()
    own_c.start()
    own_d.start()
    pc[7] = jnp.zeros((12, R), F32)

    barrier = pltpu.get_barrier_semaphore()
    for to in [sib, *near.values()]:
        pl.semaphore_signal(barrier, inc=1, device_id=to, device_id_type=MESH)
    pl.semaphore_wait(barrier, 7)

    send(u_hbm.at[pl.ds(4 * (1 - c), 4)], h.at[c], sib_s.at[0], sib_r.at[0], sib)

    def buf(m):
        return pg if m == PCH else g.at[m]

    AXES = (("x", "y"), ("y", "x"))
    at = {"x": (x, NX), "y": (y, NY)}

    def pos(axis, d):
        v, n = at[axis]
        return wrap(v + d, n)

    def piece(m, hf, k0, nk, d):
        first = AXES[hf][0]
        px = pos("x", d) if first == "x" else x
        py = pos("y", d) if first == "y" else y
        return buf(m).at[pl.ds(4 * c + 2 * hf + k0, nk), px, py]

    def line(m, hf, k0, nk, d, core=None):
        second = AXES[hf][1]
        ks = pl.ds(4 * (c if core is None else core) + 2 * hf + k0, nk)
        if second == "y":
            return buf(m).at[ks, :, pos("y", d)]
        return buf(m).at[ks, pos("x", d), :]

    def sem(m, stage, hf, i):
        n = stage * 4 + hf * 2 + i
        return ag_s.at[m, n], ag_r.at[m, n]

    def sib_sem(m, hf, i):
        n = 16 + hf * 4 + i
        return ag_s.at[m, n], ag_r.at[m, n]

    DIRS = (1, -1)

    def go(m, stage, hf, i, view, axis):
        send(view, view, *sem(m, stage, hf, i), near[(axis, DIRS[i])])

    def got(m, stage, hf, i, view):
        remote(view, view, *sem(m, stage, hf, i), sib).wait_recv()

    def to_sib(m, hf, i, d):
        view = line(m, hf, 0, 2, d)
        send(view, view, *sib_sem(m, hf, i), sib)

    def inside(m):
        return 0 <= m <= PCH

    def e0(m):
        if inside(m):
            for hf in range(2):
                for i in range(2):
                    go(m, 0, hf, i, piece(m, hf, 0, 2, 0), AXES[hf][0])

    def e1(m):
        if inside(m):
            for hf in range(2):
                for i in range(2):
                    d = -DIRS[i]
                    got(m, 0, hf, i, piece(m, hf, 0, 2, d))
                    go(m, 1, hf, i, piece(m, hf, i, 1, d), AXES[hf][0])

    def e2(m):
        if inside(m):
            for hf in range(2):
                for i in range(2):
                    got(m, 1, hf, i, piece(m, hf, i, 1, 2))
                for i in range(2):
                    go(m, 2, hf, i, line(m, hf, 0, 2, 0), AXES[hf][1])
            for hf in range(2):
                to_sib(m, hf, 0, 0)

    def e3(m):
        if inside(m):
            for hf in range(2):
                for i in range(2):
                    d = -DIRS[i]
                    got(m, 2, hf, i, line(m, hf, 0, 2, d))
                    go(m, 3, hf, i, line(m, hf, i, 1, d), AXES[hf][1])
            for hf in range(2):
                for i in range(2):
                    to_sib(m, hf, 1 + i, -DIRS[i])

    def e4(m):
        if inside(m):
            for hf in range(2):
                for i in range(2):
                    got(m, 3, hf, i, line(m, hf, i, 1, 2))
                to_sib(m, hf, 3, 2)

    def e5(m):
        if inside(m):
            for hf in range(2):
                for i, d in enumerate((0, -1, 1, 2)):
                    view = line(m, hf, 0, 2, d, 1 - c)
                    remote(view, view, *sib_sem(m, hf, i), sib).wait_recv()

    def merge(m):
        if not inside(m):
            return
        if m == PCH:
            for i in range(4):
                for s in range(2):
                    pg[4 * c + i, x, y, 12 * s : 12 * s + 12, :] = hp[s, i]
            return
        rows = lax.broadcasted_iota(jnp.int32, (12, 128), 0) + chip * 24
        for i in range(4):
            for b in range(2):
                j, bb = divmod(2 * m + b, 3)
                limit = ub[4 * c + i, j] * 128
                for s in range(2):
                    keep = (rows + 12 * s < limit).astype(F32)
                    part = h[s, i, j, :, bb * 128 : bb * 128 + 128]
                    g[m, 4 * c + i, x, y, 12 * s : 12 * s + 12, b * 128 : b * 128 + 128] = part * keep

    def convert_l(k):
        load_l(k).wait()
        p, kk = divmod(k, 2)
        for i in range(2):
            for b in range(3):
                keep = jnp.where((lb[i, k] > b) & (pr[i, k] > 0), 1.0, 0.0).astype(F32)
                hi, lo = split(ls[k % 2, i, :, b * 128 : b * 128 + 128] * keep)
                lanes = slice(kk * R + b * 128, kk * R + b * 128 + 128)
                lhi[p, i * R : i * R + R, lanes] = hi
                llo[p, i * R : i * R + R, lanes] = lo
        if k + 2 < 8:
            load_l(k + 2).start()

    def unit(m, p):
        if not 0 <= m < CHUNKS:
            return
        hi, lo = split(g[m, 2 * p : 2 * p + 2].reshape(2 * R, W))
        both = dot(lhi[p], hi) + dot(lhi[p], lo) + dot(llo[p], hi)
        both = both.reshape(2, NZ, 48, W)
        if p == 0:
            acc[m] = both
        else:
            acc[m] = acc[m] + both

    def ups(m):
        return 4 if m % 2 == 0 else 3

    def rs(m, s):
        if not 0 <= m < CHUNKS:
            return
        hu = ups(m)
        for axis_dir, n, base in ((1, hu, 0), (-1, 7 - hu, hu)):
            if s > n:
                continue
            dest = wrap(z + axis_dir * (n - s + 1), NZ)
            view = acc.at[m, :, dest]
            if s > 1:
                i = base + s - 2
                arrived = rb.at[m, i]
                remote(arrived, arrived, rs_s.at[m, i], rs_r.at[m, i], sib).wait_recv()
                acc[m, :, dest] = acc[m, :, dest] + rb[m, i]
            i = base + s - 1
            send(view, rb.at[m, i], rs_s.at[m, i], rs_r.at[m, i], near[("z", axis_dir)])

    def rs_end(m):
        if not 0 <= m < CHUNKS:
            return
        hu = ups(m)
        for i in (hu - 1, 6):
            arrived = rb.at[m, i]
            remote(arrived, arrived, rs_s.at[m, i], rs_r.at[m, i], sib).wait_recv()
        total = acc[m, :, z] + rb[m, hu - 1] + rb[m, 6]
        for b in range(2):
            j, bb = divmod(2 * m + b, 3)
            res = diag[:, j, :, bb * 128 : bb * 128 + 128] - total[:, :, b * 128 : b * 128 + 128]
            red[:, 256 * m + b * 128 : 256 * m + b * 128 + 128] = res.reshape(96, 128)

    def times(a, mat):
        ah, al = split(a)
        bh, bl = split(pg[mat].reshape(R, R))
        return dot(ah, bh) + dot(ah, bl) + dot(al, bh)

    convert_l(0)
    own_p.wait()
    own_c.wait()
    send(pc.at[pl.ds(4 * (1 - c), 4)], hp.at[c], sib_s.at[1], sib_r.at[1], sib)
    hp[c] = pc[pl.ds(4 * c, 4)]
    own_u.wait()
    remote(h.at[1 - c], h.at[1 - c], sib_s.at[0], sib_r.at[0], sib).wait_recv()
    merge(0)
    e0(0)
    merge(1)
    e0(1)
    convert_l(1)
    e1(0)
    convert_l(2)
    remote(hp.at[1 - c], hp.at[1 - c], sib_s.at[1], sib_r.at[1], sib).wait_recv()

    for s in range(PCH + 2):
        e2(s)
        e4(s - 1)
        unit(s - 2, 3)
        rs(s - 2, 1)
        rs(s - 3, 4)
        e1(s + 1)
        merge(s + 2)
        e0(s + 2)
        if s == 0:
            convert_l(3)
            convert_l(4)
        if s == 1:
            convert_l(6)
            convert_l(7)
            own_d.wait()
        e5(s - 1)
        unit(s - 1, 0)
        rs(s - 2, 2)
        e3(s)
        if s == 0:
            convert_l(5)
        unit(s - 1, 1)
        rs_end(s - 3)
        unit(s - 1, 2)
        rs(s - 2, 3)

    last = CHUNKS - 1
    rs(last, 4)
    linked = None
    for j in range(3):
        a = red[:, R * j : R * j + R]
        if linked is not None:
            a = a - linked
        done = times(a, j)
        out[:, j] = done.reshape(2, 48, R)
        linked = times(done, 4 + j)
    rs_end(last)
    out[:, 3] = times(red[:, 3 * R :] - linked, 3).reshape(2, 48, R)
    for copy in sends:
        copy.wait_send()


def per_device(l_cores, l_bucket, present, u_cores, u_bucket, diag_cores, pivot_inv, coupling):
    anyspace = pl.BlockSpec(memory_space=pl.ANY)
    smem = pl.BlockSpec(memory_space=pltpu.SMEM)
    dma = pltpu.SemaphoreType.DMA
    return pl.pallas_call(
        kernel,
        out_shape=jax.ShapeDtypeStruct((2, 4, 48, R), F32),
        in_specs=[smem, smem, smem, anyspace, anyspace, anyspace, anyspace, anyspace],
        out_specs=pl.BlockSpec(memory_space=pltpu.VMEM),
        scratch_shapes=[
            pltpu.VMEM((CHUNKS, 8, NX, NY, 24, W), F32),
            pltpu.VMEM((8, NX, NY, 24, R), F32),
            pltpu.VMEM((2, 4, 4, 12, R), F32),
            pltpu.VMEM((2, 4, 12, R), F32),
            pltpu.VMEM((8, 12, R), F32),
            pltpu.VMEM((2, 2, R, R), F32),
            pltpu.VMEM((4, 2 * R, 2 * R), BF),
            pltpu.VMEM((4, 2 * R, 2 * R), BF),
            pltpu.VMEM((CHUNKS, 2, NZ, 48, W), F32),
            pltpu.VMEM((CHUNKS, 7, 2, 48, W), F32),
            pltpu.VMEM((96, 4 * R), F32),
            pltpu.VMEM((2, 4, 48, R), F32),
            dma((4,)), dma((2,)), dma((2,)), dma((2,)),
            dma((CHUNKS + 1, 24)), dma((CHUNKS + 1, 24)),
            dma((CHUNKS, 7)), dma((CHUNKS, 7)),
        ],
        compiler_params=pltpu.CompilerParams(
            collective_id=0, has_side_effects=True, vmem_limit_bytes=60 * 2**20
        ),
    )(l_bucket, present, u_bucket, l_cores, u_cores, diag_cores, pivot_inv, coupling)


def solution(mesh):
    in_specs = (
        P("row", "depth", None, None),
        P("row", "depth"),
        P("row", "depth"),
        P("depth", None, "row", None),
        P("depth", None),
        P("row", None, "depth", None),
        P(None, "row", None),
        P(None, "row", None),
    )
    return jax.shard_map(
        per_device, mesh=mesh, in_specs=in_specs, out_specs=P("row", None, "depth", None), check_vma=False
    )
```

```python
import jax
import jax.numpy as jnp
from jax import lax
from jax.experimental import pallas as pl
from jax.experimental.pallas import tpu as pltpu
from jax.sharding import PartitionSpec as P

MESH = pl.DeviceIdType.MESH
NX, NY, NZ = 4, 4, 8
R = 384
WIDTHS = (256, 256, 256, 256, 256, 256)
N = len(WIDTHS)
FIRST = [sum(WIDTHS[:m]) // 128 for m in range(N)]
PCH = N
CUT = 3
TURNS = 4
BF, F32 = jnp.bfloat16, jnp.float32

ORDER = (
    ("mg", 0), ("e0", 0, 0), ("e0", 0, 1), ("mg", 1), ("e0", 1, 0), ("e0", 1, 1), ("mg", 2),
    ("e0", 2, 0), ("e0", 2, 1), ("mg", 3), ("e0", 3, 0), ("e0", 3, 1), ("L", 0), ("L", 1), ("L", 2),
    ("e1", 0, 1, 1), ("e1", 0, 0, 0), ("e1", 0, 1, 0), ("e1", 0, 0, 1), ("L", 3), ("e1", 1, 1, 0),
    ("e1", 1, 0, 0), ("e1", 1, 0, 1), ("e1", 1, 1, 1), ("e1", 2, 0, 0), ("e1", 2, 0, 1),
    ("e1", 2, 1, 1), ("e1", 2, 1, 0), ("L", 4), ("e1", 3, 0, 1), ("e1", 3, 1, 1), ("e1", 3, 1, 0),
    ("e1", 3, 0, 0), ("L", 5), ("e2", 0, 0), ("e2", 0, 1), ("mg", 4), ("e0", 4, 1), ("e0", 4, 0),
    ("L", 6), ("L", 7), ("e2", 1, 0), ("e2", 1, 1), ("mg", 5), ("e0", 5, 0), ("e0", 5, 1),
    ("e3", 0, 0, 0), ("e3", 0, 0, 1), ("e3", 0, 1, 1), ("e3", 0, 1, 0), ("e1", 4, 1, 0),
    ("e1", 4, 1, 1), ("e1", 4, 0, 0), ("e1", 4, 0, 1), ("e2", 2, 0), ("e2", 2, 1), ("e3", 1, 0, 0),
    ("e3", 1, 0, 1), ("e3", 1, 1, 0), ("e3", 1, 1, 1), ("e1", 5, 1, 0), ("e1", 5, 1, 1),
    ("e1", 5, 0, 0), ("e1", 5, 0, 1), ("e4", 0, 0), ("u", 0, 0, 0), ("e4", 0, 1), ("u", 0, 0, 1),
    ("e2", 3, 1), ("e2", 3, 0), ("u", 0, 0, 2), ("u", 0, 0, 3), ("r", 0, 0, 0, 1), ("r", 0, 0, 1, 1),
    ("e3", 2, 0, 1), ("e3", 2, 1, 1), ("e3", 2, 0, 0), ("e3", 2, 1, 0), ("e4", 1, 0), ("u", 1, 0, 0),
    ("e2", 4, 0), ("e2", 4, 1), ("e4", 1, 1), ("u", 1, 0, 1), ("u", 1, 0, 2), ("r", 0, 0, 1, 2),
    ("r", 0, 0, 0, 2), ("u", 1, 0, 3), ("r", 1, 0, 0, 1), ("r", 1, 0, 1, 1), ("e3", 3, 0, 1),
    ("e3", 3, 1, 1), ("e3", 3, 1, 0), ("e3", 3, 0, 0), ("e4", 2, 0), ("u", 2, 0, 0), ("e2", 5, 1),
    ("e2", 5, 0), ("e4", 2, 1), ("u", 2, 0, 1), ("r", 0, 0, 0, 3), ("r", 0, 0, 1, 3), ("u", 2, 0, 2),
    ("e3", 4, 0, 1), ("r", 1, 0, 1, 2), ("r", 1, 0, 0, 2), ("e3", 4, 1, 1), ("e3", 4, 1, 0),
    ("e3", 4, 0, 0), ("u", 2, 0, 3), ("r", 2, 0, 0, 1), ("r", 2, 0, 1, 1), ("e4", 3, 0), ("e4", 3, 1),
    ("u", 3, 0, 0), ("u", 3, 0, 1), ("mg", 6), ("r", 0, 0, 0, 4), ("e0", 6, 0), ("e0", 6, 1),
    ("u", 3, 0, 2), ("u", 3, 0, 3), ("r", 3, 0, 0, 1), ("r", 3, 0, 1, 1), ("u", 3, 1, 0),
    ("r", 1, 0, 1, 3), ("r", 1, 0, 0, 3), ("e3", 5, 0, 0), ("e3", 5, 1, 1), ("e3", 5, 1, 0),
    ("e3", 5, 0, 1), ("u", 3, 1, 1), ("u", 3, 1, 2), ("r", 2, 0, 1, 2), ("r", 2, 0, 0, 2),
    ("e4", 4, 1), ("e4", 4, 0), ("u", 3, 1, 3), ("r", 3, 1, 1, 1), ("r", 3, 1, 0, 1),
    ("r", 3, 0, 1, 2), ("u", 4, 0, 0), ("e1", 6, 1, 0), ("e1", 6, 0, 0), ("e1", 6, 0, 1),
    ("e1", 6, 1, 1), ("u", 4, 0, 1), ("r", 3, 0, 0, 2), ("u", 4, 0, 2), ("r", 1, 0, 1, 4),
    ("u", 4, 0, 3), ("r", 4, 0, 1, 1), ("r", 4, 0, 0, 1), ("e4", 5, 0), ("e4", 5, 1), ("u", 4, 1, 0),
    ("u", 4, 1, 1), ("r", 2, 0, 1, 3), ("e2", 6, 0), ("e2", 6, 1), ("u", 4, 1, 2), ("r", 3, 1, 1, 2),
    ("r", 2, 0, 0, 3), ("u", 4, 1, 3), ("r", 3, 0, 1, 3), ("r", 4, 1, 1, 1), ("r", 3, 1, 0, 2),
    ("r", 4, 1, 0, 1), ("u", 5, 0, 0), ("u", 5, 0, 1), ("r", 3, 0, 0, 3), ("u", 5, 0, 2),
    ("u", 5, 0, 3), ("r", 5, 0, 1, 1), ("r", 4, 0, 0, 2), ("r", 4, 0, 1, 2), ("r", 5, 0, 0, 1),
    ("u", 5, 1, 0), ("u", 5, 1, 1), ("u", 5, 1, 2), ("r", 2, 0, 0, 4), ("u", 5, 1, 3),
    ("r", 5, 1, 0, 1), ("r", 3, 1, 0, 3), ("r", 5, 1, 1, 1), ("re", 0, 0), ("re", 1, 0),
    ("r", 3, 1, 1, 3), ("r", 4, 1, 0, 2), ("r", 3, 0, 1, 4), ("e3", 6, 0, 0), ("e3", 6, 0, 1),
    ("e3", 6, 1, 1), ("e3", 6, 1, 0), ("r", 4, 1, 1, 2), ("r", 4, 0, 0, 3), ("r", 5, 0, 1, 2),
    ("r", 5, 0, 0, 2), ("r", 4, 0, 1, 3), ("r", 5, 1, 1, 2), ("re", 2, 0), ("r", 3, 1, 1, 4),
    ("r", 5, 1, 0, 2), ("re", 3, 0), ("e4", 6, 0), ("e4", 6, 1), ("r", 4, 1, 1, 3), ("r", 4, 1, 0, 3),
    ("r", 5, 0, 1, 3), ("r", 4, 0, 0, 4), ("F", 0), ("r", 5, 1, 1, 3), ("r", 5, 0, 0, 3), ("F", 1),
    ("r", 4, 1, 0, 4), ("r", 5, 1, 0, 3), ("re", 3, 1), ("re", 4, 0), ("r", 5, 0, 1, 4),
    ("r", 5, 1, 1, 4), ("re", 4, 1), ("F", 2), ("re", 5, 0), ("re", 5, 1), ("F", 3),
)


def split(a):
    hi = a.astype(BF)
    return hi, (a - hi.astype(F32)).astype(BF)


def dot(a, b):
    return jnp.dot(a, b, preferred_element_type=F32)


def parts(m):
    return 2 if m >= CUT else 1


def kernel(
    lb, pr, ub, l_hbm, u_hbm, d_hbm, p_hbm, c_hbm,
    out,
    gs, pg, h, us, hp, pc, pv, ls, lhi, llo, accs, rbs, red, diag, carry,
    lsem, lssem, sib_s, sib_r, ag_s, ag_r, rs_s, rs_r,
):
    row = lax.axis_index("row")
    z = lax.axis_index("depth")
    x, y, c = row // 8, (row // 2) % 4, row % 2
    chip = x * 4 + y

    def dev(xx, yy, cc, zz):
        return ((xx * 4 + yy) * 2 + cc, zz)

    def wrap(v, n):
        return (v + n) % n

    sib = dev(x, y, 1 - c, z)
    near = {
        ("x", 1): dev(wrap(x + 1, NX), y, c, z), ("x", -1): dev(wrap(x - 1, NX), y, c, z),
        ("y", 1): dev(x, wrap(y + 1, NY), c, z), ("y", -1): dev(x, wrap(y - 1, NY), c, z),
        ("z", 1): dev(x, y, c, wrap(z + 1, NZ)), ("z", -1): dev(x, y, c, wrap(z - 1, NZ)),
    }

    pending = {}

    def remote(src, dst, ssem, rsem, to):
        return pltpu.make_async_remote_copy(
            src_ref=src, dst_ref=dst, send_sem=ssem, recv_sem=rsem, device_id=to, device_id_type=MESH
        )

    def send(src, dst, key, rsem, to):
        sem, at = key
        if key in pending:
            pending.pop(key).wait_send()
        copy = remote(src, dst, (sib_s, ag_s, rs_s)[sem].at[at], rsem, to)
        copy.start()
        pending[key] = copy

    def got(view, rsem):
        remote(view, view, sib_s.at[0], rsem, sib).wait_recv()

    def load_l(k):
        return pltpu.make_async_copy(l_hbm.at[:, k], ls.at[k % 2], lssem.at[k % 2])

    own_u = pltpu.make_async_copy(u_hbm.at[pl.ds(4 * c, 4)], h.at[c], lsem.at[0])
    own_p = pltpu.make_async_copy(p_hbm, pv, lsem.at[1])
    own_c = pltpu.make_async_copy(c_hbm, pc.at[pl.ds(4, 3)], lsem.at[2])
    own_d = pltpu.make_async_copy(d_hbm, diag, lsem.at[3])
    give_u = pltpu.make_async_copy(u_hbm.at[pl.ds(4 * (1 - c), 4)], us, lsem.at[4])
    give_u.start()
    own_u.start()
    own_p.start()
    own_c.start()
    load_l(0).start()
    load_l(1).start()
    own_d.start()

    barrier = pltpu.get_barrier_semaphore()
    for to in [sib, *near.values()]:
        pl.semaphore_signal(barrier, inc=1, device_id=to, device_id_type=MESH)
    pc[7] = jnp.zeros((12, R), F32)
    own_p.wait()
    own_c.wait()
    for i in range(4):
        pc[i] = pv[:, i, :]
    give_u.wait()
    pl.semaphore_wait(barrier, 7)

    send(us, h.at[c], (0, 0), sib_r.at[0], sib)
    send(pc.at[pl.ds(4 * (1 - c), 4)], hp.at[c], (0, 1), sib_r.at[1], sib)
    hp[c] = pc[pl.ds(4 * c, 4)]

    def buf(m):
        return pg if m == PCH else gs[m]

    AXES = (("x", "y"), ("y", "x"))
    DIRS = (1, -1)
    at = {"x": (x, NX), "y": (y, NY)}

    def pos(axis, d):
        v, n = at[axis]
        return wrap(v + d, n)

    def piece(m, hf, k0, nk, d):
        first = AXES[hf][0]
        px = pos("x", d) if first == "x" else x
        py = pos("y", d) if first == "y" else y
        return buf(m).at[pl.ds(4 * c + 2 * hf + k0, nk), px, py]

    def line(m, hf, k0, nk, d, core=None):
        second = AXES[hf][1]
        ks = pl.ds(4 * (c if core is None else core) + 2 * hf + k0, nk)
        if second == "y":
            return buf(m).at[ks, :, pos("y", d)]
        return buf(m).at[ks, pos("x", d), :]

    def sems(m, n):
        return (1, (m % TURNS, n)), ag_r.at[m, n]

    def go(m, stage, hf, i, view):
        to = near[(AXES[hf][stage // 2], DIRS[i])]
        send(view, view, *sems(m, stage * 4 + hf * 2 + i), to)

    def come(m, stage, hf, i, view):
        got(view, sems(m, stage * 4 + hf * 2 + i)[1])

    def to_sib(m, hf, i, d):
        view = line(m, hf, 0, 2, d)
        send(view, view, *sems(m, 16 + hf * 4 + i), sib)

    def from_sib(m, hf):
        for i, d in enumerate((0, -1, 1, 2)):
            got(line(m, hf, 0, 2, d, 1 - c), sems(m, 16 + hf * 4 + i)[1])

    def e0(m, hf):
        for i in range(2):
            go(m, 0, hf, i, piece(m, hf, 0, 2, 0))

    def e1(m, hf, i):
        d = -DIRS[i]
        come(m, 0, hf, i, piece(m, hf, 0, 2, d))
        go(m, 1, hf, i, piece(m, hf, i, 1, d))

    def e2(m, hf):
        for i in range(2):
            come(m, 1, hf, i, piece(m, hf, i, 1, 2))
        for i in range(2):
            go(m, 2, hf, i, line(m, hf, 0, 2, 0))
        to_sib(m, hf, 0, 0)

    def e3(m, hf, i):
        d = -DIRS[i]
        come(m, 2, hf, i, line(m, hf, 0, 2, d))
        go(m, 3, hf, i, line(m, hf, i, 1, d))
        to_sib(m, hf, 1 + i, d)

    def e4(m, hf):
        for i in range(2):
            come(m, 3, hf, i, line(m, hf, i, 1, 2))
        to_sib(m, hf, 3, 2)

    def mg(m):
        if m == 0:
            own_u.wait()
            got(h.at[1 - c], sib_r.at[0])
        if m == PCH:
            got(hp.at[1 - c], sib_r.at[1])
            for i in range(4):
                for s in range(2):
                    pg[4 * c + i, x, y, 12 * s : 12 * s + 12, :] = hp[s, i]
            return
        rows = lax.broadcasted_iota(jnp.int32, (12, 128), 0) + chip * 24
        for i in range(4):
            for b in range(WIDTHS[m] // 128):
                j, bb = divmod(FIRST[m] + b, 3)
                limit = ub[j, 4 * c + i] * 128
                for s in range(2):
                    keep = (rows + 12 * s < limit).astype(F32)
                    part = h[s, i, :, j, bb * 128 : bb * 128 + 128]
                    gs[m][4 * c + i, x, y, 12 * s : 12 * s + 12, b * 128 : b * 128 + 128] = part * keep

    def convert_l(k):
        load_l(k).wait()
        p, kk = divmod(k, 2)
        for i in range(2):
            for b in range(3):
                keep = jnp.where((lb[i, k] > b) & (pr[i, k] > 0), 1.0, 0.0).astype(F32)
                hi, lo = split(ls[k % 2, i, :, b * 128 : b * 128 + 128] * keep)
                lanes = slice(kk * R + b * 128, kk * R + b * 128 + 128)
                lhi[p, i * R : i * R + R, lanes] = hi
                llo[p, i * R : i * R + R, lanes] = lo
        if k + 2 < 8:
            load_l(k + 2).start()

    def unit(m, i, q):
        w, hf, core = WIDTHS[m], q % 2, c if q < 2 else 1 - c
        if q >= 2 and i == 0:
            from_sib(m, hf)
        p = 2 * core + hf
        rows, shape = slice(0, 2 * R), (2, NZ, 48, w)
        dest = accs[m].at[...]
        if parts(m) == 2:
            rows, shape = slice(i * R, i * R + R), (NZ, 48, w)
            dest = accs[m].at[i]
        hi, lo = split(gs[m][pl.ds(2 * p, 2)].reshape(2 * R, w))
        if w == 128:
            both = dot(lhi[p, rows], jnp.concatenate([hi, lo], axis=1))
            res = both[:, :128] + both[:, 128:] + dot(llo[p, rows], hi)
        else:
            res = dot(lhi[p, rows], hi) + dot(lhi[p, rows], lo) + dot(llo[p, rows], hi)
        res = res.reshape(shape)
        dest[...] = res if q == 0 else dest[...] + res

    def hops(m):
        up = 4 if m % 2 == 0 else 3
        return ((1, up, 0), (-1, 7 - up, up))

    def rviews(m, i, dest):
        return accs[m].at[:, dest] if parts(m) == 1 else accs[m].at[i, dest]

    def rbuf(m, i, n):
        return rbs[m].at[n] if parts(m) == 1 else rbs[m].at[n, i]

    def rsem(m, i, n):
        sums = m if i == 0 else N + m - CUT
        return (2, (sums % TURNS, n)), rs_r.at[sums, n]

    def rs(m, i, d, st):
        way, n, base = hops(m)[d]
        view = rviews(m, i, wrap(z + way * (n - st + 1), NZ))
        if st > 1:
            arrived = rbuf(m, i, base + st - 2)
            got(arrived, rsem(m, i, base + st - 2)[1])
            view[...] = view[...] + arrived[...]
        k = base + st - 1
        send(view, rbuf(m, i, k), *rsem(m, i, k), near[("z", way)])

    def rs_end(m, i):
        total = rviews(m, i, z)[...]
        for way, n, base in hops(m):
            arrived = rbuf(m, i, base + n - 1)
            got(arrived, rsem(m, i, base + n - 1)[1])
            total = total + arrived[...]
        for b in range(WIDTHS[m] // 128):
            j, bb = divmod(FIRST[m] + b, 3)
            lanes, own = slice(bb * 128, bb * 128 + 128), slice(b * 128, b * 128 + 128)
            to = slice((FIRST[m] + b) * 128, (FIRST[m] + b) * 128 + 128)
            if parts(m) == 1:
                red[:, to] = (diag[:, j, :, lanes] - total[:, :, own]).reshape(96, 128)
            else:
                red[48 * i : 48 * i + 48, to] = diag[i, j, :, lanes] - total[:, own]

    def times(a, mat):
        ah, al = split(a)
        bh, bl = split(pg[mat].reshape(R, R))
        return dot(ah, bh) + dot(ah, bl) + dot(al, bh)

    def finish(j):
        if j == 0:
            for hf in range(2):
                from_sib(PCH, hf)
        a = red[:, R * j : R * j + R]
        if j > 0:
            a = a - carry[...]
        done = times(a, j)
        out[:, j] = done.reshape(2, 48, R)
        if j < 3:
            carry[...] = times(done, 4 + j)

    steps = dict(
        mg=mg, e0=e0, e1=e1, e2=e2, e3=e3, e4=e4, L=convert_l, u=unit, r=rs, re=rs_end, F=finish
    )
    waited = False
    for name, *args in ORDER:
        if name == "re" and not waited:
            own_d.wait()
            waited = True
        steps[name](*args)
    for copy in pending.values():
        copy.wait_send()


def per_device(l_cores, l_bucket, present, u_cores, u_bucket, diag_cores, pivot_inv, coupling):
    anyspace = pl.BlockSpec(memory_space=pl.ANY)
    smem = pl.BlockSpec(memory_space=pltpu.SMEM)
    dma = pltpu.SemaphoreType.DMA
    vmem = pltpu.VMEM
    return pl.pallas_call(
        kernel,
        out_shape=jax.ShapeDtypeStruct((2, 4, 48, R), F32),
        in_specs=[smem, smem, smem, anyspace, anyspace, anyspace, anyspace, anyspace],
        out_specs=pl.BlockSpec(memory_space=vmem),
        scratch_shapes=[
            [vmem((8, NX, NY, 24, w), F32) for w in WIDTHS],
            vmem((8, NX, NY, 24, R), F32),
            vmem((2, 4, 12, 4, R), F32),
            vmem((4, 12, 4, R), F32),
            vmem((2, 4, 12, R), F32),
            vmem((8, 12, R), F32),
            vmem((12, 4, R), F32),
            vmem((2, 2, R, R), F32),
            vmem((4, 2 * R, 2 * R), BF),
            vmem((4, 2 * R, 2 * R), BF),
            [vmem((2, NZ, 48, w), F32) for w in WIDTHS],
            [vmem((7, 2, 48, w), F32) for w in WIDTHS],
            vmem((96, 4 * R), F32),
            vmem((2, 4, 48, R), F32),
            vmem((96, R), F32),
            dma((5,)), dma((2,)), dma((2,)), dma((2,)),
            dma((TURNS, 24)), dma((N + 1, 24)),
            dma((TURNS, 7)), dma((2 * N - CUT, 7)),
        ],
        compiler_params=pltpu.CompilerParams(
            collective_id=0, has_side_effects=True, vmem_limit_bytes=60 * 2**20
        ),
    )(
        l_bucket, present, u_bucket.T, l_cores, u_cores.transpose(0, 2, 1, 3), diag_cores,
        pivot_inv.transpose(1, 0, 2), coupling,
    )


def solution(mesh):
    in_specs = (
        P("row", "depth", None, None),
        P("row", "depth"),
        P("row", "depth"),
        P("depth", None, "row", None),
        P("depth", None),
        P("row", None, "depth", None),
        P(None, "row", None),
        P(None, "row", None),
    )
    return jax.shard_map(
        per_device, mesh=mesh, in_specs=in_specs, out_specs=P("row", None, "depth", None), check_vma=False
    )
```

```python
import jax
import jax.numpy as jnp
from jax import lax
from jax.experimental import pallas as pl
from jax.experimental.pallas import tpu as pltpu
from jax.sharding import PartitionSpec as P

MESH = pl.DeviceIdType.MESH
NX, NY, NZ = 4, 4, 8
R = 384
WIDTHS = (128, 128, 128, 128, 256, 256, 256, 256)
N = len(WIDTHS)
FIRST = [sum(WIDTHS[:m]) // 128 for m in range(N)]
PCH = N
CUT = 2
DIRECT = 1
TREE = (0, 0, 1, 1, 0, 0, 0, 0)
TURNS = 4
BF, F32 = jnp.bfloat16, jnp.float32

ORDER = (
    ("mg", 0), ("e0", 0, 0), ("e0", 0, 1), ("mg", 1), ("e0", 1, 1), ("e0", 1, 0), ("mg", 2),
    ("e0", 2, 1), ("e0", 2, 0), ("mg", 3), ("e0", 3, 0), ("e0", 3, 1), ("mg", 4), ("e0", 4, 0),
    ("e0", 4, 1), ("L", 0), ("L", 1), ("L", 2), ("e1", 1, 0, 1), ("e1", 1, 1, 1), ("e1", 1, 0, 0),
    ("e1", 1, 1, 0), ("e2", 0, 0), ("e1", 2, 1, 1), ("e1", 2, 1, 0), ("e1", 2, 0, 0), ("e1", 2, 0, 1),
    ("e2", 0, 1), ("e1", 3, 1, 1), ("e1", 3, 0, 0), ("e1", 3, 0, 1), ("e1", 3, 1, 0), ("mg", 5),
    ("e0", 5, 0), ("e0", 5, 1), ("e1", 4, 0, 1), ("e1", 4, 1, 0), ("e1", 4, 1, 1), ("e1", 4, 0, 0),
    ("L", 3), ("L", 4), ("L", 5), ("e2", 1, 0), ("e2", 1, 1), ("e3", 0, 0, 0), ("e3", 0, 0, 1),
    ("mg", 6), ("e0", 6, 1), ("e3", 0, 1, 0), ("e3", 0, 1, 1), ("e0", 6, 0), ("L", 6), ("L", 7),
    ("e4", 0, 0), ("e2", 2, 0), ("e2", 2, 1), ("mg", 7), ("e4", 0, 1), ("e0", 7, 0), ("e1", 5, 1, 1),
    ("e0", 7, 1), ("e1", 5, 0, 0), ("e1", 5, 0, 1), ("e1", 5, 1, 0), ("u", 0, 0, 0), ("u", 0, 0, 1),
    ("u", 0, 0, 2), ("e3", 1, 0, 0), ("e3", 1, 1, 1), ("e3", 1, 1, 0), ("e3", 1, 0, 1), ("u", 0, 0, 3),
    ("r", 0, 0, 0, 1), ("r", 0, 0, 1, 1), ("e2", 3, 1), ("e2", 3, 0), ("e1", 6, 0, 1), ("e1", 6, 0, 0),
    ("e1", 6, 1, 1), ("e1", 6, 1, 0), ("e3", 2, 0, 1), ("e3", 2, 0, 0), ("e3", 2, 1, 0),
    ("e3", 2, 1, 1), ("e1", 7, 1, 0), ("e1", 7, 0, 0), ("e1", 7, 0, 1), ("e1", 7, 1, 1), ("e2", 4, 0),
    ("e2", 4, 1), ("r", 0, 0, 0, 2), ("r", 0, 0, 1, 2), ("e4", 1, 0), ("u", 1, 0, 0), ("e4", 1, 1),
    ("u", 1, 0, 1), ("u", 1, 0, 2), ("e3", 3, 1, 1), ("e3", 3, 0, 1), ("e3", 3, 1, 0), ("e3", 3, 0, 0),
    ("u", 1, 0, 3), ("r", 1, 0, 0, 1), ("r", 0, 0, 0, 3), ("r", 0, 0, 1, 3), ("r", 1, 0, 1, 1),
    ("e4", 2, 0), ("e4", 2, 1), ("e2", 5, 0), ("u", 2, 0, 0), ("e2", 5, 1), ("u", 2, 0, 1),
    ("u", 2, 0, 2), ("u", 2, 0, 3), ("r", 2, 0, 1, 1), ("r", 2, 0, 0, 1), ("u", 2, 1, 0),
    ("u", 2, 1, 1), ("u", 2, 1, 2), ("u", 2, 1, 3), ("r", 1, 0, 0, 2), ("r", 2, 1, 0, 1),
    ("r", 2, 1, 1, 1), ("e3", 4, 0, 1), ("e3", 4, 1, 1), ("e3", 4, 1, 0), ("r", 0, 0, 0, 4),
    ("e3", 4, 0, 0), ("r", 1, 0, 1, 2), ("e4", 3, 0), ("u", 3, 0, 0), ("r", 2, 0, 1, 2), ("e4", 3, 1),
    ("u", 3, 0, 1), ("e2", 6, 0), ("e2", 6, 1), ("u", 3, 0, 2), ("r", 2, 0, 0, 2), ("r", 2, 1, 1, 2),
    ("u", 3, 0, 3), ("r", 1, 0, 0, 3), ("r", 3, 0, 0, 1), ("r", 3, 0, 1, 1), ("u", 3, 1, 0),
    ("u", 3, 1, 1), ("r", 1, 0, 1, 3), ("e3", 5, 0, 1), ("e3", 5, 0, 0), ("e3", 5, 1, 0),
    ("e3", 5, 1, 1), ("u", 3, 1, 2), ("r", 2, 1, 0, 2), ("u", 3, 1, 3), ("r", 3, 1, 0, 1),
    ("r", 3, 1, 1, 1), ("e4", 4, 0), ("re", 0, 0), ("u", 4, 0, 0), ("e4", 4, 1), ("u", 4, 0, 1),
    ("e2", 7, 0), ("e2", 7, 1), ("re", 2, 0), ("u", 4, 0, 2), ("u", 4, 0, 3), ("r", 3, 0, 0, 2),
    ("r", 3, 0, 1, 2), ("r", 4, 0, 0, 1), ("r", 4, 0, 1, 1), ("u", 4, 1, 0), ("r", 1, 0, 1, 4),
    ("e3", 6, 0, 1), ("e3", 6, 0, 0), ("u", 4, 1, 1), ("r", 3, 1, 0, 2), ("e3", 6, 1, 1),
    ("e3", 6, 1, 0), ("re", 2, 1), ("u", 4, 1, 2), ("r", 3, 1, 1, 2), ("u", 4, 1, 3),
    ("r", 4, 1, 0, 1), ("r", 4, 1, 1, 1), ("e4", 5, 1), ("e4", 5, 0), ("u", 5, 0, 0), ("u", 5, 0, 1),
    ("re", 3, 0), ("mg", 8), ("r", 4, 0, 1, 2), ("r", 4, 0, 0, 2), ("e0", 8, 1), ("e0", 8, 0),
    ("u", 5, 0, 2), ("re", 1, 0), ("u", 5, 0, 3), ("r", 5, 0, 0, 1), ("r", 5, 0, 1, 1), ("u", 5, 1, 0),
    ("r", 4, 1, 0, 2), ("e3", 7, 1, 1), ("e3", 7, 1, 0), ("e3", 7, 0, 0), ("e3", 7, 0, 1),
    ("r", 4, 1, 1, 2), ("re", 3, 1), ("u", 5, 1, 1), ("u", 5, 1, 2), ("r", 4, 0, 0, 3),
    ("r", 4, 0, 1, 3), ("e4", 6, 0), ("e4", 6, 1), ("u", 5, 1, 3), ("r", 5, 1, 1, 1),
    ("r", 5, 1, 0, 1), ("u", 6, 0, 0), ("r", 5, 0, 1, 2), ("r", 5, 0, 0, 2), ("e1", 8, 0, 0),
    ("e1", 8, 1, 1), ("e1", 8, 0, 1), ("e1", 8, 1, 0), ("u", 6, 0, 1), ("r", 4, 1, 0, 3),
    ("r", 4, 1, 1, 3), ("u", 6, 0, 2), ("e4", 7, 1), ("e4", 7, 0), ("u", 6, 0, 3), ("r", 4, 0, 0, 4),
    ("r", 6, 0, 0, 1), ("r", 6, 0, 1, 1), ("u", 6, 1, 0), ("r", 5, 1, 0, 2), ("r", 5, 1, 1, 2),
    ("u", 6, 1, 1), ("u", 6, 1, 2), ("r", 5, 0, 0, 3), ("r", 5, 0, 1, 3), ("u", 6, 1, 3),
    ("r", 4, 1, 0, 4), ("r", 6, 1, 1, 1), ("r", 6, 1, 0, 1), ("u", 7, 0, 0), ("e2", 8, 0),
    ("e2", 8, 1), ("r", 6, 0, 1, 2), ("re", 4, 0), ("u", 7, 0, 1), ("u", 7, 0, 2), ("r", 5, 1, 1, 3),
    ("r", 6, 0, 0, 2), ("u", 7, 0, 3), ("r", 5, 1, 0, 3), ("r", 5, 0, 1, 4), ("r", 7, 0, 1, 1),
    ("r", 7, 0, 0, 1), ("u", 7, 1, 0), ("u", 7, 1, 1), ("r", 6, 1, 1, 2), ("u", 7, 1, 2),
    ("r", 6, 0, 1, 3), ("re", 4, 1), ("u", 7, 1, 3), ("r", 6, 1, 0, 2), ("r", 7, 1, 1, 1),
    ("r", 7, 1, 0, 1), ("r", 5, 1, 1, 4), ("r", 6, 0, 0, 3), ("re", 5, 0), ("r", 7, 0, 1, 2),
    ("r", 7, 0, 0, 2), ("r", 6, 1, 1, 3), ("e3", 8, 0, 0), ("e3", 8, 0, 1), ("e3", 8, 1, 0),
    ("e3", 8, 1, 1), ("r", 6, 1, 0, 3), ("r", 7, 1, 0, 2), ("r", 7, 1, 1, 2), ("r", 6, 0, 0, 4),
    ("re", 5, 1), ("r", 7, 0, 0, 3), ("r", 7, 0, 1, 3), ("r", 6, 1, 0, 4), ("r", 7, 1, 0, 3),
    ("r", 7, 1, 1, 3), ("e4", 8, 0), ("e4", 8, 1), ("re", 6, 0), ("r", 7, 0, 1, 4), ("F", 0),
    ("r", 7, 1, 1, 4), ("re", 6, 1), ("F", 1), ("F", 2), ("re", 7, 0), ("re", 7, 1), ("F", 3),
)


def split(a):
    hi = a.astype(BF)
    return hi, (a - hi.astype(F32)).astype(BF)


def dot(a, b):
    return jnp.dot(a, b, preferred_element_type=F32)


def parts(m):
    return 2 if m >= CUT else 1


def kernel(
    lb_hbm, pr_hbm, ub_hbm, l_hbm, u_hbm, d_hbm, p_hbm, c_hbm,
    out,
    gs, pg, h, us, hp, pc, pv, ls, lhi, llo, accs, rbs, red, diag, carry, lb, pr, ub,
    lsem, lssem, sib_s, sib_r, ag_s, ag_r, rs_s, rs_r,
):
    row = lax.axis_index("row")
    z = lax.axis_index("depth")
    x, y, c = row // 8, (row // 2) % 4, row % 2
    chip = x * 4 + y

    def dev(xx, yy, cc, zz):
        return ((xx * 4 + yy) * 2 + cc, zz)

    def wrap(v, n):
        return (v + n) % n

    sib = dev(x, y, 1 - c, z)
    near = {}
    for d in (1, -1, 2):
        near["x", d] = dev(wrap(x + d, NX), y, c, z)
        near["y", d] = dev(x, wrap(y + d, NY), c, z)
    for d in (1, -1, 2, -2):
        near["z", d] = dev(x, y, c, wrap(z + d, NZ))

    pending = {}

    def remote(src, dst, ssem, rsem, to):
        return pltpu.make_async_remote_copy(
            src_ref=src, dst_ref=dst, send_sem=ssem, recv_sem=rsem, device_id=to, device_id_type=MESH
        )

    def send(src, dst, key, rsem, to):
        sem, at = key
        if key in pending:
            pending.pop(key).wait_send()
        copy = remote(src, dst, (sib_s, ag_s, rs_s)[sem].at[at], rsem, to)
        copy.start()
        pending[key] = copy

    def got(view, rsem):
        remote(view, view, sib_s.at[0], rsem, sib).wait_recv()

    def load_l(k):
        return pltpu.make_async_copy(l_hbm.at[:, k], ls.at[k % 2], lssem.at[k % 2])

    own_u = pltpu.make_async_copy(u_hbm.at[pl.ds(4 * c, 4)], h.at[c], lsem.at[0])
    own_p = pltpu.make_async_copy(p_hbm, pv, lsem.at[1])
    own_c = pltpu.make_async_copy(c_hbm, pc.at[pl.ds(4, 3)], lsem.at[2])
    own_d = pltpu.make_async_copy(d_hbm, diag, lsem.at[3])
    give_u = pltpu.make_async_copy(u_hbm.at[pl.ds(4 * (1 - c), 4)], us, lsem.at[4])
    give_u.start()
    tables = [
        pltpu.make_async_copy(src, dst, lsem.at[5 + i])
        for i, (src, dst) in enumerate(((ub_hbm, ub), (lb_hbm, lb), (pr_hbm, pr)))
    ]
    for table in tables:
        table.start()
    own_u.start()
    own_p.start()
    own_c.start()
    load_l(0).start()
    load_l(1).start()
    own_d.start()

    barrier = pltpu.get_barrier_semaphore()
    for to in [sib, *near.values()]:
        pl.semaphore_signal(barrier, inc=1, device_id=to, device_id_type=MESH)
    pc[7] = jnp.zeros((12, R), F32)
    own_p.wait()
    own_c.wait()
    for i in range(4):
        pc[i] = pv[:, i, :]
    give_u.wait()
    pl.semaphore_wait(barrier, 1 + len(near))

    send(us, h.at[c], (0, 0), sib_r.at[0], sib)
    send(pc.at[pl.ds(4 * (1 - c), 4)], hp.at[c], (0, 1), sib_r.at[1], sib)
    hp[c] = pc[pl.ds(4 * c, 4)]

    def buf(m):
        return pg if m == PCH else gs[m]

    AXES = (("x", "y"), ("y", "x"))
    DIRS = (1, -1)
    at = {"x": (x, NX), "y": (y, NY)}

    def pos(axis, d):
        v, n = at[axis]
        return wrap(v + d, n)

    def piece(m, hf, k0, nk, d):
        first = AXES[hf][0]
        px = pos("x", d) if first == "x" else x
        py = pos("y", d) if first == "y" else y
        return buf(m).at[pl.ds(4 * c + 2 * hf + k0, nk), px, py]

    def line(m, hf, k0, nk, d, core=None):
        second = AXES[hf][1]
        ks = pl.ds(4 * (c if core is None else core) + 2 * hf + k0, nk)
        if second == "y":
            return buf(m).at[ks, :, pos("y", d)]
        return buf(m).at[ks, pos("x", d), :]

    def sems(m, n):
        return (1, (m % TURNS, n)), ag_r.at[m, n]

    def go(m, stage, hf, i, view):
        to = near[(AXES[hf][stage // 2], DIRS[i])]
        send(view, view, *sems(m, stage * 4 + hf * 2 + i), to)

    def far(m, stage, hf, view):
        send(view, view, *sems(m, stage * 4 + hf * 2), near[AXES[hf][stage // 2], 2])

    def come(m, stage, hf, i, view):
        got(view, sems(m, stage * 4 + hf * 2 + i)[1])

    def to_sib(m, hf, i, d):
        view = line(m, hf, 0, 2, d)
        send(view, view, *sems(m, 16 + hf * 4 + i), sib)

    def from_sib(m, hf):
        for i, d in enumerate((0, -1, 1, 2)):
            got(line(m, hf, 0, 2, d, 1 - c), sems(m, 16 + hf * 4 + i)[1])

    def e0(m, hf):
        view = piece(m, hf, 0, 2, 0)
        for i in range(2):
            go(m, 0, hf, i, view)
        if m < DIRECT:
            far(m, 1, hf, view)

    def e1(m, hf, i):
        d = -DIRS[i]
        come(m, 0, hf, i, piece(m, hf, 0, 2, d))
        go(m, 1, hf, i, piece(m, hf, i, 1, d))

    def e2(m, hf):
        if m < DIRECT:
            for i in range(2):
                come(m, 0, hf, i, piece(m, hf, 0, 2, -DIRS[i]))
            come(m, 1, hf, 0, piece(m, hf, 0, 2, 2))
        else:
            for i in range(2):
                come(m, 1, hf, i, piece(m, hf, i, 1, 2))
        for i in range(2):
            go(m, 2, hf, i, line(m, hf, 0, 2, 0))
        if m < DIRECT:
            far(m, 3, hf, line(m, hf, 0, 2, 0))
        to_sib(m, hf, 0, 0)

    def e3(m, hf, i):
        d = -DIRS[i]
        come(m, 2, hf, i, line(m, hf, 0, 2, d))
        if m >= DIRECT:
            go(m, 3, hf, i, line(m, hf, i, 1, d))
        to_sib(m, hf, 1 + i, d)

    def e4(m, hf):
        if m < DIRECT:
            come(m, 3, hf, 0, line(m, hf, 0, 2, 2))
        else:
            for i in range(2):
                come(m, 3, hf, i, line(m, hf, i, 1, 2))
        to_sib(m, hf, 3, 2)

    def mg(m):
        if m == 0:
            own_u.wait()
            for table in tables:
                table.wait()
            got(h.at[1 - c], sib_r.at[0])
        if m == PCH:
            got(hp.at[1 - c], sib_r.at[1])
            for i in range(4):
                for s in range(2):
                    pg[4 * c + i, x, y, 12 * s : 12 * s + 12, :] = hp[s, i]
            return
        rows = lax.broadcasted_iota(jnp.int32, (12, 128), 0) + chip * 24
        for i in range(4):
            for b in range(WIDTHS[m] // 128):
                j, bb = divmod(FIRST[m] + b, 3)
                limit = ub[j, 4 * c + i] * 128
                for s in range(2):
                    keep = (rows + 12 * s < limit).astype(F32)
                    part = h[s, i, :, j, bb * 128 : bb * 128 + 128]
                    gs[m][4 * c + i, x, y, 12 * s : 12 * s + 12, b * 128 : b * 128 + 128] = part * keep

    def convert_l(k):
        load_l(k).wait()
        p, kk = divmod(k, 2)
        for i in range(2):
            for b in range(3):
                keep = jnp.where((lb[i, k] > b) & (pr[i, k] > 0), 1.0, 0.0).astype(F32)
                hi, lo = split(ls[k % 2, i, :, b * 128 : b * 128 + 128] * keep)
                lanes = slice(kk * R + b * 128, kk * R + b * 128 + 128)
                lhi[p, i * R : i * R + R, lanes] = hi
                llo[p, i * R : i * R + R, lanes] = lo
        if k + 2 < 8:
            load_l(k + 2).start()

    def unit(m, i, q):
        w, hf, core = WIDTHS[m], q % 2, c if q < 2 else 1 - c
        if q >= 2 and i == 0:
            from_sib(m, hf)
        p = 2 * core + hf
        rows, shape = slice(0, 2 * R), (2, NZ, 48, w)
        dest = accs[m].at[...]
        if parts(m) == 2:
            rows, shape = slice(i * R, i * R + R), (NZ, 48, w)
            dest = accs[m].at[i]
        hi, lo = split(gs[m][pl.ds(2 * p, 2)].reshape(2 * R, w))
        if w == 128:
            both = dot(lhi[p, rows], jnp.concatenate([hi, lo], axis=1))
            res = both[:, :128] + both[:, 128:] + dot(llo[p, rows], hi)
        else:
            res = dot(lhi[p, rows], hi) + dot(lhi[p, rows], lo) + dot(llo[p, rows], hi)
        res = res.reshape(shape)
        dest[...] = res if q == 0 else dest[...] + res

    def hops(m):
        up = 4 if m % 2 == 0 else 3
        return ((1, up, 0), (-1, 7 - up, up))

    def rviews(m, i, dest):
        return accs[m].at[:, dest] if parts(m) == 1 else accs[m].at[i, dest]

    def rbuf(m, i, n):
        return rbs[m].at[n] if parts(m) == 1 else rbs[m].at[n, i]

    def rsem(m, i, n):
        sums = m if i == 0 else N + m - CUT
        return (2, (sums % TURNS, n)), rs_r.at[sums, n]

    def pass_on(m, i, k, dest, way, steps):
        send(rviews(m, i, dest), rbuf(m, i, k), *rsem(m, i, k), near["z", way * steps])

    def tree(m, i, d, st):
        way, n, _ = hops(m)[d]
        base = 3 * d
        if st == 1:
            pass_on(m, i, base + 1, wrap(z + 3 * way, NZ), way, 1)
            if n == 4:
                pass_on(m, i, 6, wrap(z + 4 * way, NZ), way, 2)
            pass_on(m, i, base, wrap(z + way, NZ), way, 1)
            return
        dest = wrap(z + 2 * way, NZ)
        view = rviews(m, i, dest)
        for k in (base + 1, 6)[: n - 2]:
            got(rbuf(m, i, k), rsem(m, i, k)[1])
            view[...] = view[...] + rbuf(m, i, k)[...]
        pass_on(m, i, base + 2, dest, way, 2)

    def rs(m, i, d, st):
        if TREE[m]:
            tree(m, i, d, st)
            return
        way, n, base = hops(m)[d]
        view = rviews(m, i, wrap(z + way * (n - st + 1), NZ))
        if st > 1:
            arrived = rbuf(m, i, base + st - 2)
            got(arrived, rsem(m, i, base + st - 2)[1])
            view[...] = view[...] + arrived[...]
        k = base + st - 1
        send(view, rbuf(m, i, k), *rsem(m, i, k), near[("z", way)])

    def rs_end(m, i):
        total = rviews(m, i, z)[...]
        ends = (0, 2, 3, 5) if TREE[m] else [base + n - 1 for _, n, base in hops(m)]
        for k in ends:
            arrived = rbuf(m, i, k)
            got(arrived, rsem(m, i, k)[1])
            total = total + arrived[...]
        for b in range(WIDTHS[m] // 128):
            j, bb = divmod(FIRST[m] + b, 3)
            lanes, own = slice(bb * 128, bb * 128 + 128), slice(b * 128, b * 128 + 128)
            to = slice((FIRST[m] + b) * 128, (FIRST[m] + b) * 128 + 128)
            if parts(m) == 1:
                red[:, to] = (diag[:, j, :, lanes] - total[:, :, own]).reshape(96, 128)
            else:
                red[48 * i : 48 * i + 48, to] = diag[i, j, :, lanes] - total[:, own]

    def times(a, mat):
        ah, al = split(a)
        bh, bl = split(pg[mat].reshape(R, R))
        return dot(ah, bh) + dot(ah, bl) + dot(al, bh)

    def finish(j):
        if j == 0:
            for hf in range(2):
                from_sib(PCH, hf)
        a = red[:, R * j : R * j + R]
        if j > 0:
            a = a - carry[...]
        done = times(a, j)
        out[:, j] = done.reshape(2, 48, R)
        if j < 3:
            carry[...] = times(done, 4 + j)

    steps = dict(
        mg=mg, e0=e0, e1=e1, e2=e2, e3=e3, e4=e4, L=convert_l, u=unit, r=rs, re=rs_end, F=finish
    )
    waited = False
    for name, *args in ORDER:
        if name == "re" and not waited:
            own_d.wait()
            waited = True
        steps[name](*args)
    for copy in pending.values():
        copy.wait_send()


def per_device(l_cores, l_bucket, present, u_cores, u_bucket, diag_cores, pivot_inv, coupling):
    anyspace = pl.BlockSpec(memory_space=pl.ANY)
    smem = pltpu.SMEM
    dma = pltpu.SemaphoreType.DMA
    vmem = pltpu.VMEM
    return pl.pallas_call(
        kernel,
        out_shape=jax.ShapeDtypeStruct((2, 4, 48, R), F32),
        in_specs=[anyspace, anyspace, anyspace, anyspace, anyspace, anyspace, anyspace, anyspace],
        out_specs=pl.BlockSpec(memory_space=vmem),
        scratch_shapes=[
            [vmem((8, NX, NY, 24, w), F32) for w in WIDTHS],
            vmem((8, NX, NY, 24, R), F32),
            vmem((2, 4, 12, 4, R), F32),
            vmem((4, 12, 4, R), F32),
            vmem((2, 4, 12, R), F32),
            vmem((8, 12, R), F32),
            vmem((12, 4, R), F32),
            vmem((2, 2, R, R), F32),
            vmem((4, 2 * R, 2 * R), BF),
            vmem((4, 2 * R, 2 * R), BF),
            [vmem((2, NZ, 48, w), F32) for w in WIDTHS],
            [vmem((7, 2, 48, w), F32) for w in WIDTHS],
            vmem((96, 4 * R), F32),
            vmem((2, 4, 48, R), F32),
            vmem((96, R), F32),
            smem((2, 8), jnp.int32), smem((2, 8), jnp.int32), smem((4, 8), jnp.int32),
            dma((8,)), dma((2,)), dma((2,)), dma((2,)),
            dma((TURNS, 24)), dma((N + 1, 24)),
            dma((TURNS, 7)), dma((2 * N - CUT, 7)),
        ],
        compiler_params=pltpu.CompilerParams(
            collective_id=0, has_side_effects=True, vmem_limit_bytes=60 * 2**20
        ),
    )(
        l_bucket, present, u_bucket.T, l_cores, u_cores.transpose(0, 2, 1, 3), diag_cores,
        pivot_inv.transpose(1, 0, 2), coupling,
    )


def solution(mesh):
    in_specs = (
        P("row", "depth", None, None),
        P("row", "depth"),
        P("row", "depth"),
        P("depth", None, "row", None),
        P("depth", None),
        P("row", None, "depth", None),
        P(None, "row", None),
        P(None, "row", None),
    )
    return jax.shard_map(
        per_device, mesh=mesh, in_specs=in_specs, out_specs=P("row", None, "depth", None), check_vma=False
    )
```

```python
import jax
import jax.numpy as jnp
from jax import lax
from jax.experimental import pallas as pl
from jax.experimental.pallas import tpu as pltpu
from jax.sharding import PartitionSpec as P

MESH = pl.DeviceIdType.MESH
NX, NY, NZ = 4, 4, 8
R = 384
WIDTHS = (128, 128, 256, 256, 256, 256, 256)
N = len(WIDTHS)
FIRST = [sum(WIDTHS[:m]) // 128 for m in range(N)]
PCH = N
CUT = 5
DIRECT = 1
TREE = (1, 0, 0, 0, 0, 0, 0)
TURNS = 4
BF, F32 = jnp.bfloat16, jnp.float32

ORDER = (
    ("mg", 0), ("mg", 1), ("mg", 2), ("e0", 0, 0), ("e0", 0, 1), ("mg", 3), ("mg", 4), ("e0", 1, 0),
    ("e0", 1, 1), ("e0", 2, 0), ("e0", 2, 1), ("e0", 3, 0), ("e0", 3, 1), ("e0", 4, 0), ("e0", 4, 1),
    ("L", 0), ("L", 1), ("L", 2), ("e1", 1, 0, 0), ("e1", 1, 0, 1), ("e2", 0, 0), ("e2", 0, 1),
    ("e1", 1, 1, 0), ("e1", 1, 1, 1), ("mg", 5), ("e1", 2, 0, 0), ("e1", 2, 0, 1), ("e1", 2, 1, 0),
    ("e1", 2, 1, 1), ("e0", 5, 0), ("e0", 5, 1), ("L", 3), ("e1", 3, 0, 0), ("e1", 3, 0, 1),
    ("e1", 3, 1, 0), ("e1", 3, 1, 1), ("L", 4), ("e1", 4, 0, 0), ("e1", 4, 0, 1), ("e1", 4, 1, 0),
    ("e1", 4, 1, 1), ("L", 5), ("L", 6), ("e3", 0, 0, 0), ("e3", 0, 0, 1), ("e3", 0, 1, 0),
    ("e3", 0, 1, 1), ("e2", 1, 0), ("L", 7), ("e2", 1, 1), ("mg", 6), ("e4", 0, 0), ("e4", 0, 1),
    ("e2", 2, 0), ("e2", 2, 1), ("e0", 6, 0), ("e0", 6, 1), ("u", 0, 0, 0), ("e1", 5, 0, 0),
    ("e1", 5, 0, 1), ("e1", 5, 1, 0), ("e1", 5, 1, 1), ("u", 0, 0, 1), ("u", 0, 0, 2), ("u", 0, 0, 3),
    ("r", 0, 0, 0, 1), ("r", 0, 0, 1, 1), ("e3", 1, 0, 0), ("e3", 1, 0, 1), ("e3", 1, 1, 0),
    ("e3", 1, 1, 1), ("e2", 3, 0), ("e2", 3, 1), ("e3", 2, 0, 0), ("r", 0, 0, 1, 2), ("e3", 2, 0, 1),
    ("e3", 2, 1, 0), ("e3", 2, 1, 1), ("e1", 6, 1, 0), ("e1", 6, 1, 1), ("e1", 6, 0, 0),
    ("e1", 6, 0, 1), ("r", 0, 0, 0, 2), ("e4", 1, 0), ("u", 1, 0, 0), ("e4", 1, 1), ("e2", 4, 0),
    ("e2", 4, 1), ("u", 1, 0, 1), ("u", 1, 0, 2), ("u", 1, 0, 3), ("r", 1, 0, 0, 1), ("r", 1, 0, 1, 1),
    ("e3", 3, 0, 0), ("e3", 3, 0, 1), ("e3", 3, 1, 0), ("e3", 3, 1, 1), ("re", 0, 0), ("e4", 2, 0),
    ("u", 2, 0, 0), ("e4", 2, 1), ("e2", 5, 0), ("e2", 5, 1), ("r", 1, 0, 0, 2), ("r", 1, 0, 1, 2),
    ("u", 2, 0, 1), ("u", 2, 0, 2), ("u", 2, 0, 3), ("r", 2, 0, 0, 1), ("r", 2, 0, 1, 1),
    ("e3", 4, 0, 0), ("e3", 4, 0, 1), ("e3", 4, 1, 0), ("e3", 4, 1, 1), ("r", 1, 0, 0, 3),
    ("r", 1, 0, 1, 3), ("e4", 3, 0), ("u", 3, 0, 0), ("e4", 3, 1), ("e2", 6, 0), ("e2", 6, 1),
    ("u", 3, 0, 1), ("u", 3, 0, 2), ("r", 2, 0, 0, 2), ("r", 2, 0, 1, 2), ("e3", 5, 0, 0),
    ("e3", 5, 0, 1), ("r", 1, 0, 1, 4), ("e3", 5, 1, 0), ("e3", 5, 1, 1), ("u", 3, 0, 3),
    ("r", 3, 0, 0, 1), ("r", 3, 0, 1, 1), ("mg", 7), ("e4", 4, 0), ("e4", 4, 1), ("e0", 7, 0),
    ("e0", 7, 1), ("u", 4, 0, 0), ("u", 4, 0, 1), ("r", 2, 0, 0, 3), ("r", 2, 0, 1, 3), ("u", 4, 0, 2),
    ("e3", 6, 0, 0), ("e3", 6, 0, 1), ("e3", 6, 1, 0), ("e3", 6, 1, 1), ("r", 3, 0, 0, 2),
    ("re", 1, 0), ("u", 4, 0, 3), ("r", 3, 0, 1, 2), ("r", 4, 0, 0, 1), ("r", 4, 0, 1, 1),
    ("e4", 5, 0), ("e4", 5, 1), ("u", 5, 0, 0), ("u", 5, 0, 1), ("e1", 7, 1, 0), ("e1", 7, 1, 1),
    ("r", 2, 0, 0, 4), ("e1", 7, 0, 0), ("e1", 7, 0, 1), ("u", 5, 0, 2), ("u", 5, 0, 3),
    ("r", 5, 0, 0, 1), ("r", 5, 0, 1, 1), ("u", 5, 1, 0), ("r", 3, 0, 0, 3), ("e4", 6, 0),
    ("e4", 6, 1), ("u", 5, 1, 1), ("u", 5, 1, 2), ("r", 3, 0, 1, 3), ("e2", 7, 1), ("e2", 7, 0),
    ("r", 4, 0, 0, 2), ("u", 5, 1, 3), ("r", 5, 1, 0, 1), ("r", 5, 1, 1, 1), ("u", 6, 0, 0),
    ("r", 4, 0, 1, 2), ("u", 6, 0, 1), ("re", 2, 0), ("r", 5, 0, 1, 2), ("u", 6, 0, 2),
    ("r", 5, 0, 0, 2), ("u", 6, 0, 3), ("r", 6, 0, 0, 1), ("r", 6, 0, 1, 1), ("u", 6, 1, 0),
    ("u", 6, 1, 1), ("r", 3, 0, 1, 4), ("u", 6, 1, 2), ("r", 5, 1, 1, 2), ("u", 6, 1, 3),
    ("r", 6, 1, 0, 1), ("r", 6, 1, 1, 1), ("r", 4, 0, 0, 3), ("r", 4, 0, 1, 3), ("r", 5, 1, 0, 2),
    ("r", 5, 0, 1, 3), ("e3", 7, 1, 0), ("e3", 7, 1, 1), ("e3", 7, 0, 0), ("r", 5, 0, 0, 3),
    ("e3", 7, 0, 1), ("r", 6, 0, 1, 2), ("r", 6, 0, 0, 2), ("r", 6, 1, 0, 2), ("re", 3, 0),
    ("r", 5, 1, 1, 3), ("r", 4, 0, 0, 4), ("r", 6, 1, 1, 2), ("r", 5, 1, 0, 3), ("e4", 7, 1),
    ("e4", 7, 0), ("r", 6, 0, 0, 3), ("r", 5, 0, 1, 4), ("F", 0), ("r", 6, 0, 1, 3), ("r", 6, 1, 0, 3),
    ("r", 5, 1, 1, 4), ("F", 1), ("r", 6, 1, 1, 3), ("re", 4, 0), ("re", 5, 0), ("r", 6, 0, 0, 4),
    ("r", 6, 1, 0, 4), ("re", 5, 1), ("F", 2), ("re", 6, 0), ("re", 6, 1), ("F", 3),
)


def split(a):
    hi = a.astype(BF)
    return hi, (a - hi.astype(F32)).astype(BF)


def dot(a, b):
    return jnp.dot(a, b, preferred_element_type=F32)


def parts(m):
    return 2 if m >= CUT else 1


def kernel(
    lb_hbm, pr_hbm, ub_hbm, l_hbm, u_hbm, d_hbm, p_hbm, c_hbm,
    out,
    gs, pg, h, us, hp, pc, pv, ls, lhi, llo, accs, rbs, red, diag, carry, done_v, lb, pr, ub,
    lsem, lssem, sib_s, sib_r, ag_s, ag_r, rs_s, rs_r,
):
    row = lax.axis_index("row")
    z = lax.axis_index("depth")
    x, y, c = row // 8, (row // 2) % 4, row % 2
    chip = x * 4 + y

    def dev(xx, yy, cc, zz):
        return ((xx * 4 + yy) * 2 + cc, zz)

    def wrap(v, n):
        return (v + n) % n

    sib = dev(x, y, 1 - c, z)
    near = {}
    for d in (1, -1, 2):
        near["x", d] = dev(wrap(x + d, NX), y, c, z)
        near["y", d] = dev(x, wrap(y + d, NY), c, z)
    for d in (1, -1, 2, -2):
        near["z", d] = dev(x, y, c, wrap(z + d, NZ))

    pending = {}

    def remote(src, dst, ssem, rsem, to):
        return pltpu.make_async_remote_copy(
            src_ref=src, dst_ref=dst, send_sem=ssem, recv_sem=rsem, device_id=to, device_id_type=MESH
        )

    def send(src, dst, key, rsem, to):
        sem, at = key
        if key in pending:
            pending.pop(key).wait_send()
        copy = remote(src, dst, (sib_s, ag_s, rs_s)[sem].at[at], rsem, to)
        copy.start()
        pending[key] = copy

    def got(view, rsem):
        remote(view, view, sib_s.at[0], rsem, sib).wait_recv()

    def load_l(k):
        return pltpu.make_async_copy(l_hbm.at[:, k], ls.at[k % 2], lssem.at[k % 2])

    own_u = pltpu.make_async_copy(u_hbm.at[pl.ds(4 * c, 4)], h.at[c], lsem.at[0])
    own_p = pltpu.make_async_copy(p_hbm, pv, lsem.at[1])
    own_c = pltpu.make_async_copy(c_hbm, pc.at[pl.ds(4, 3)], lsem.at[2])
    own_d = pltpu.make_async_copy(d_hbm, diag, lsem.at[3])
    give_u = pltpu.make_async_copy(u_hbm.at[pl.ds(4 * (1 - c), 4)], us, lsem.at[4])
    give_u.start()
    tables = [
        pltpu.make_async_copy(src, dst, lsem.at[5 + i])
        for i, (src, dst) in enumerate(((ub_hbm, ub), (lb_hbm, lb), (pr_hbm, pr)))
    ]
    for table in tables:
        table.start()
    own_u.start()
    own_p.start()
    own_c.start()
    load_l(0).start()
    load_l(1).start()
    own_d.start()

    barrier = pltpu.get_barrier_semaphore()
    for to in [sib, *near.values()]:
        pl.semaphore_signal(barrier, inc=1, device_id=to, device_id_type=MESH)
    pc[7] = jnp.zeros((12, R), F32)
    own_p.wait()
    own_c.wait()
    for i in range(4):
        pc[i] = pv[:, i, :]
    give_u.wait()
    pl.semaphore_wait(barrier, 1 + len(near))

    send(us, h.at[c], (0, 0), sib_r.at[0], sib)
    send(pc.at[pl.ds(4 * (1 - c), 4)], hp.at[c], (0, 1), sib_r.at[1], sib)
    hp[c] = pc[pl.ds(4 * c, 4)]

    def buf(m):
        return pg if m == PCH else gs[m]

    AXES = (("x", "y"), ("y", "x"))
    DIRS = (1, -1)
    at = {"x": (x, NX), "y": (y, NY)}

    def pos(axis, d):
        v, n = at[axis]
        return wrap(v + d, n)

    def piece(m, hf, k0, nk, d):
        first = AXES[hf][0]
        px = pos("x", d) if first == "x" else x
        py = pos("y", d) if first == "y" else y
        return buf(m).at[pl.ds(4 * c + 2 * hf + k0, nk), px, py]

    def line(m, hf, k0, nk, d, core=None):
        second = AXES[hf][1]
        ks = pl.ds(4 * (c if core is None else core) + 2 * hf + k0, nk)
        if second == "y":
            return buf(m).at[ks, :, pos("y", d)]
        return buf(m).at[ks, pos("x", d), :]

    def sems(m, n):
        return (1, (m % TURNS, n)), ag_r.at[m, n]

    def go(m, stage, hf, i, view):
        to = near[(AXES[hf][stage // 2], DIRS[i])]
        send(view, view, *sems(m, stage * 4 + hf * 2 + i), to)

    def far(m, stage, hf, view):
        send(view, view, *sems(m, stage * 4 + hf * 2), near[AXES[hf][stage // 2], 2])

    def come(m, stage, hf, i, view):
        got(view, sems(m, stage * 4 + hf * 2 + i)[1])

    def to_sib(m, hf, i, d):
        view = line(m, hf, 0, 2, d)
        send(view, view, *sems(m, 16 + hf * 4 + i), sib)

    def from_sib(m, hf):
        for i, d in enumerate((0, -1, 1, 2)):
            got(line(m, hf, 0, 2, d, 1 - c), sems(m, 16 + hf * 4 + i)[1])

    def e0(m, hf):
        view = piece(m, hf, 0, 2, 0)
        for i in range(2):
            go(m, 0, hf, i, view)
        if m < DIRECT:
            far(m, 1, hf, view)

    def e1(m, hf, i):
        d = -DIRS[i]
        come(m, 0, hf, i, piece(m, hf, 0, 2, d))
        go(m, 1, hf, i, piece(m, hf, i, 1, d))

    def e2(m, hf):
        if m < DIRECT:
            for i in range(2):
                come(m, 0, hf, i, piece(m, hf, 0, 2, -DIRS[i]))
            come(m, 1, hf, 0, piece(m, hf, 0, 2, 2))
        else:
            for i in range(2):
                come(m, 1, hf, i, piece(m, hf, i, 1, 2))
        for i in range(2):
            go(m, 2, hf, i, line(m, hf, 0, 2, 0))
        if m < DIRECT:
            far(m, 3, hf, line(m, hf, 0, 2, 0))
        to_sib(m, hf, 0, 0)

    def e3(m, hf, i):
        d = -DIRS[i]
        come(m, 2, hf, i, line(m, hf, 0, 2, d))
        if m >= DIRECT:
            go(m, 3, hf, i, line(m, hf, i, 1, d))
        to_sib(m, hf, 1 + i, d)

    def e4(m, hf):
        if m < DIRECT:
            come(m, 3, hf, 0, line(m, hf, 0, 2, 2))
        else:
            for i in range(2):
                come(m, 3, hf, i, line(m, hf, i, 1, 2))
        to_sib(m, hf, 3, 2)

    def mg(m):
        if m == 0:
            own_u.wait()
            for table in tables:
                table.wait()
            got(h.at[1 - c], sib_r.at[0])
        if m == PCH:
            got(hp.at[1 - c], sib_r.at[1])
            for i in range(4):
                for s in range(2):
                    pg[4 * c + i, x, y, 12 * s : 12 * s + 12, :] = hp[s, i]
            return
        rows = lax.broadcasted_iota(jnp.int32, (12, 128), 0) + chip * 24
        for i in range(4):
            for b in range(WIDTHS[m] // 128):
                j, bb = divmod(FIRST[m] + b, 3)
                limit = ub[j, 4 * c + i] * 128
                for s in range(2):
                    keep = (rows + 12 * s < limit).astype(F32)
                    part = h[s, i, :, j, bb * 128 : bb * 128 + 128]
                    gs[m][4 * c + i, x, y, 12 * s : 12 * s + 12, b * 128 : b * 128 + 128] = part * keep

    def convert_l(k):
        load_l(k).wait()
        p, kk = divmod(k, 2)
        for i in range(2):
            for b in range(3):
                keep = jnp.where((lb[i, k] > b) & (pr[i, k] > 0), 1.0, 0.0).astype(F32)
                hi, lo = split(ls[k % 2, i, :, b * 128 : b * 128 + 128] * keep)
                lanes = slice(kk * R + b * 128, kk * R + b * 128 + 128)
                lhi[p, i * R : i * R + R, lanes] = hi
                llo[p, i * R : i * R + R, lanes] = lo
        if k + 2 < 8:
            load_l(k + 2).start()

    def unit(m, i, q):
        w, hf, core = WIDTHS[m], q % 2, c if q < 2 else 1 - c
        if q >= 2 and i == 0:
            from_sib(m, hf)
        p = 2 * core + hf
        rows, shape = slice(0, 2 * R), (2, NZ, 48, w)
        dest = accs[m].at[...]
        if parts(m) == 2:
            rows, shape = slice(i * R, i * R + R), (NZ, 48, w)
            dest = accs[m].at[i]
        hi, lo = split(gs[m][pl.ds(2 * p, 2)].reshape(2 * R, w))
        if w == 128:
            both = dot(lhi[p, rows], jnp.concatenate([hi, lo], axis=1))
            res = both[:, :128] + both[:, 128:] + dot(llo[p, rows], hi)
        else:
            res = dot(lhi[p, rows], hi) + dot(lhi[p, rows], lo) + dot(llo[p, rows], hi)
        res = res.reshape(shape)
        dest[...] = res if q == 0 else dest[...] + res

    def hops(m):
        up = 4 if m % 2 == 0 else 3
        return ((1, up, 0), (-1, 7 - up, up))

    def rviews(m, i, dest):
        return accs[m].at[:, dest] if parts(m) == 1 else accs[m].at[i, dest]

    def rbuf(m, i, n):
        return rbs[m].at[n] if parts(m) == 1 else rbs[m].at[n, i]

    def rsem(m, i, n):
        sums = m if i == 0 else N + m - CUT
        return (2, (sums % TURNS, n)), rs_r.at[sums, n]

    def pass_on(m, i, k, dest, way, steps):
        send(rviews(m, i, dest), rbuf(m, i, k), *rsem(m, i, k), near["z", way * steps])

    def tree(m, i, d, st):
        way, n, _ = hops(m)[d]
        base = 3 * d
        if st == 1:
            pass_on(m, i, base + 1, wrap(z + 3 * way, NZ), way, 1)
            if n == 4:
                pass_on(m, i, 6, wrap(z + 4 * way, NZ), way, 2)
            pass_on(m, i, base, wrap(z + way, NZ), way, 1)
            return
        dest = wrap(z + 2 * way, NZ)
        view = rviews(m, i, dest)
        for k in (base + 1, 6)[: n - 2]:
            got(rbuf(m, i, k), rsem(m, i, k)[1])
            view[...] = view[...] + rbuf(m, i, k)[...]
        pass_on(m, i, base + 2, dest, way, 2)

    def rs(m, i, d, st):
        if TREE[m]:
            tree(m, i, d, st)
            return
        way, n, base = hops(m)[d]
        view = rviews(m, i, wrap(z + way * (n - st + 1), NZ))
        if st > 1:
            arrived = rbuf(m, i, base + st - 2)
            got(arrived, rsem(m, i, base + st - 2)[1])
            view[...] = view[...] + arrived[...]
        k = base + st - 1
        send(view, rbuf(m, i, k), *rsem(m, i, k), near[("z", way)])

    def rs_end(m, i):
        total = rviews(m, i, z)[...]
        ends = (0, 2, 3, 5) if TREE[m] else [base + n - 1 for _, n, base in hops(m)]
        for k in ends:
            arrived = rbuf(m, i, k)
            got(arrived, rsem(m, i, k)[1])
            total = total + arrived[...]
        for b in range(WIDTHS[m] // 128):
            j, bb = divmod(FIRST[m] + b, 3)
            lanes, own = slice(bb * 128, bb * 128 + 128), slice(b * 128, b * 128 + 128)
            to = slice((FIRST[m] + b) * 128, (FIRST[m] + b) * 128 + 128)
            if parts(m) == 1:
                red[:, to] = (diag[:, j, :, lanes] - total[:, :, own]).reshape(96, 128)
            else:
                red[48 * i : 48 * i + 48, to] = diag[i, j, :, lanes] - total[:, own]

    def times(a, mat):
        ah, al = split(a)
        bh, bl = split(pg[mat].reshape(R, R))
        return dot(ah, bh) + dot(ah, bl) + dot(al, bh)

    stores = []

    def finish(j):
        if j == 0:
            for hf in range(2):
                from_sib(PCH, hf)
        a = red[:, R * j : R * j + R]
        if j > 0:
            a = a - carry[...]
        done = times(a, j)
        done_v[:, j] = done.reshape(2, 48, R)
        stores.append(pltpu.make_async_copy(done_v.at[:, j], out.at[:, j], lsem.at[8 + j]))
        stores[-1].start()
        if j < 3:
            carry[...] = times(done, 4 + j)

    steps = dict(
        mg=mg, e0=e0, e1=e1, e2=e2, e3=e3, e4=e4, L=convert_l, u=unit, r=rs, re=rs_end, F=finish
    )
    waited = False
    for name, *args in ORDER:
        if name == "re" and not waited:
            own_d.wait()
            waited = True
        steps[name](*args)
    for copy in pending.values():
        copy.wait_send()
    for copy in stores:
        copy.wait()


def per_device(l_cores, l_bucket, present, u_cores, u_bucket, diag_cores, pivot_inv, coupling):
    anyspace = pl.BlockSpec(memory_space=pl.ANY)
    smem = pltpu.SMEM
    dma = pltpu.SemaphoreType.DMA
    vmem = pltpu.VMEM
    return pl.pallas_call(
        kernel,
        out_shape=jax.ShapeDtypeStruct((2, 4, 48, R), F32),
        in_specs=[anyspace, anyspace, anyspace, anyspace, anyspace, anyspace, anyspace, anyspace],
        out_specs=anyspace,
        scratch_shapes=[
            [vmem((8, NX, NY, 24, w), F32) for w in WIDTHS],
            vmem((8, NX, NY, 24, R), F32),
            vmem((2, 4, 12, 4, R), F32),
            vmem((4, 12, 4, R), F32),
            vmem((2, 4, 12, R), F32),
            vmem((8, 12, R), F32),
            vmem((12, 4, R), F32),
            vmem((2, 2, R, R), F32),
            vmem((4, 2 * R, 2 * R), BF),
            vmem((4, 2 * R, 2 * R), BF),
            [vmem((2, NZ, 48, w), F32) for w in WIDTHS],
            [vmem((7, 2, 48, w), F32) for w in WIDTHS],
            vmem((96, 4 * R), F32),
            vmem((2, 4, 48, R), F32),
            vmem((96, R), F32),
            vmem((2, 4, 48, R), F32),
            smem((2, 8), jnp.int32), smem((2, 8), jnp.int32), smem((4, 8), jnp.int32),
            dma((12,)), dma((2,)), dma((2,)), dma((2,)),
            dma((TURNS, 24)), dma((N + 1, 24)),
            dma((TURNS, 7)), dma((2 * N - CUT, 7)),
        ],
        compiler_params=pltpu.CompilerParams(
            collective_id=0, has_side_effects=True, vmem_limit_bytes=60 * 2**20
        ),
    )(
        l_bucket, present, u_bucket.T, l_cores, u_cores.transpose(0, 2, 1, 3), diag_cores,
        pivot_inv.transpose(1, 0, 2), coupling,
    )


def solution(mesh):
    in_specs = (
        P("row", "depth", None, None),
        P("row", "depth"),
        P("row", "depth"),
        P("depth", None, "row", None),
        P("depth", None),
        P("row", None, "depth", None),
        P(None, "row", None),
        P(None, "row", None),
    )
    return jax.shard_map(
        per_device, mesh=mesh, in_specs=in_specs, out_specs=P("row", None, "depth", None), check_vma=False
    )
```
